512 devices in a mesh: ctx: 64 (over y, x, z_lo), tp: 8 (over z_hi, core).
Axes of the slice: x: 4, y: 4, z: 16 (z_hi: 4, z_lo: 4; z = z_hi * 4 + z_lo), core: 2. Of those that a mesh axis runs over, the one named last changes fastest.
Arguments:
- tokens: bfloat16 [1920, 32768], P('tp', 'ctx'), may hold values from -6 to 6
- norm_gain: float32 [1920], replicated, may hold values from 0.1 to 1.9
- w_in: bfloat16 [3, 1920, 1920], P(None, 'tp'), may hold values from -0.125 to 0.125
- w_short: float32 [3, 3, 1920], P(None, None, 'tp'), may hold values from -3 to 3
- decay_rate: float32 [16, 1920], P(None, 'tp'), as said below
- residue: float32 [16, 1920], P(None, 'tp'), may hold values from -1.5 to 1.5
- skip_gain: float32 [1920], P('tp'), may hold values from -3 to 3
- w_out: bfloat16 [1920, 1920], P('tp'), may hold values from -0.125 to 0.125
Outputs:
- mixed: bfloat16 [1920, 32768], P('tp', 'ctx')
The draws below stay inside these ranges and needn't reach their ends.
Inputs may be any that keep to these rules, and one draw needn't show every extreme that they name: `decay_rate`: every rate lies between 0.2 / 32768 and 1 / 30.
All inputs are finite; a program needn't handle non-finite values.
Results may differ from the reference program's by a relative error of at most 0.0077.
Values may be sent and summed in bfloat16 or wider, within the bound.
A program may use at most 64 MiB of HBM per device.

```python
import math
import jax
import jax.numpy as jnp
from jax import lax

D = 1920
SHORT = 3
NMODES = 16
SEQ = 32768


def draw_decay_rate(key, part):
    first, second, third = jax.random.split(jax.random.fold_in(key, 17), 3)
    shape = (NMODES, D)
    slow_share = 0.5
    slow_pick = jax.random.uniform(first, shape, jnp.float32) < slow_share
    slow_rate = jnp.exp(jax.random.uniform(second, shape, jnp.float32, math.log(0.2 / SEQ), math.log(2.0 / SEQ)))
    fast_rate = jnp.exp(jax.random.uniform(third, shape, jnp.float32, math.log(1.0 / 50.0), math.log(1.0 / 30.0)))
    return jnp.where(slow_pick, slow_rate, fast_rate).astype(jnp.float32)


def shard_levels(stream_key, extent, cuts, least, high):
    level, own = 1.0, jax.random.fold_in(stream_key, 6)
    for axis_at, parts in cuts:
        draws = jnp.exp(jax.random.uniform(jax.random.fold_in(own, axis_at), (parts,), jnp.float32, least / len(cuts), high / len(cuts)))
        level = level * jnp.repeat(draws, extent[axis_at] // parts).reshape([-1 if axis == axis_at else 1 for axis in range(len(extent))])
    return level


def bell_draw(own_key, extent, scale, most, cuts=(), kind=jnp.bfloat16):
    entries = jax.random.normal(own_key, extent, jnp.float32) * scale
    if len(cuts) > 0:
        entries = shard_levels(own_key, extent, cuts, -0.22, 0.18) * entries
    return jnp.clip(entries, min=-most, max=most).astype(kind)


def setup_inputs(seed: int = 0) -> dict:
    key_of = jax.random.split(jax.random.key(seed), 9)
    return {
        "tokens": bell_draw(key_of[0], (D, SEQ), 1.0, 6.0, ((0, 8), (1, 64))),
        "norm_gain": jnp.clip(1.0 + 0.18 * jax.random.normal(key_of[1], (D,), jnp.float32), 0.1, 1.9),
        "w_in": bell_draw(key_of[2], (3, D, D), D ** -0.5, 0.125, ((1, 8),)),
        "w_short": bell_draw(key_of[3], (SHORT, 3, D), 0.5, 3.0, ((2, 8),), jnp.float32),
        "decay_rate": draw_decay_rate(jax.random.fold_in(key_of[8], 71), 0),
        "residue": bell_draw(key_of[5], (NMODES, D), NMODES ** -0.5, 1.5, ((1, 8),), jnp.float32),
        "skip_gain": bell_draw(key_of[6], (D,), 0.5, 3.0, ((0, 8),), jnp.float32),
        "w_out": bell_draw(key_of[7], (D, D), D ** -0.5, 0.125, ((0, 8),)),
    }


def reference(tokens, norm_gain, w_in, w_short, decay_rate, residue, skip_gain, w_out):
    features = tokens.astype(jnp.float32).T
    row_scale = lax.rsqrt(lax.optimization_barrier(jnp.mean(features * features, axis=1, keepdims=True)) + 1e-06)
    normed = (features * row_scale * norm_gain).astype(jnp.bfloat16)
    w_matrix = w_in.transpose(2, 0, 1).reshape(D, 3 * D).astype(jnp.float32)
    projected = jnp.dot(normed.astype(jnp.float32), w_matrix, precision=lax.Precision.HIGHEST).astype(jnp.bfloat16)
    streams = projected.reshape(SEQ, 3, D).astype(jnp.float32)
    short_mix = w_short[0] * streams
    for offset in range(1, SHORT):
        delayed = jnp.concatenate([jnp.zeros((offset, 3, D), jnp.float32), streams[:SEQ - offset]], axis=0)
        short_mix = short_mix + w_short[offset] * delayed
    signal = short_mix[:, 1] * short_mix[:, 2]
    mode_gains = residue * jnp.sqrt(-jnp.expm1(-2.0 * decay_rate))
    group = math.gcd(D, 128)
    block_count = D // group

    def one_block(pack):
        piece, rate, gain = pack
        positions = jnp.arange(SEQ).astype(rate.dtype)
        filter_time = lax.optimization_barrier(jnp.sum(gain[None] * jnp.exp(-rate[None] * positions[:, None, None]), axis=1))
        spectrum = jnp.fft.rfft(piece, n=2 * SEQ, axis=0) * jnp.fft.rfft(filter_time, n=2 * SEQ, axis=0)
        return jnp.fft.irfft(spectrum, n=2 * SEQ, axis=0)[:SEQ]
    pieces = signal.reshape(SEQ, block_count, group).transpose(1, 0, 2)
    rates = decay_rate.reshape(NMODES, block_count, group).transpose(1, 0, 2)
    gain_blocks = mode_gains.reshape(NMODES, block_count, group).transpose(1, 0, 2)
    long_conv = lax.map(one_block, (pieces, rates, gain_blocks)).transpose(1, 0, 2).reshape(SEQ, D)
    gated = (short_mix[:, 0] * (long_conv + skip_gain * signal)).astype(jnp.bfloat16)
    result = jnp.dot(gated.astype(jnp.float32), w_out.astype(jnp.float32), precision=lax.Precision.HIGHEST)
    return result.T.astype(jnp.bfloat16)
```

```python
import functools

import jax
import jax.numpy as jnp
from jax import lax
from jax.experimental import pallas as pl
from jax.experimental.pallas import tpu as pltpu
from jax.sharding import PartitionSpec as P

MESH = pl.DeviceIdType.MESH
F32 = jnp.float32
BF16 = jnp.bfloat16
RING = 4
LINE = 4
LANES = 128
SUBS = 8


def aligned(value, step):
    return pl.multiple_of(value, step)


def mixer_kernel(
    sizes,
    tokens,
    gain,
    w_in,
    w_short,
    decay,
    residue,
    skip,
    w_out,
    out,
    feat,
    win,
    gmat,
    norm,
    proj,
    sig,
    qry,
    gat,
    taps,
    rates,
    gains,
    skips,
    ends,
    starts,
    own_state,
    line_state,
    line_total,
    totals,
    wraw,
    wturn,
    wsib,
    gown,
    gsib,
    far_out,
    far_in,
    up_out,
    up_in,
    down_out,
    down_in,
    held,
    mine,
    local_sem,
    gather_send,
    gather_recv,
    halo_send,
    halo_recv,
    wsib_send,
    wsib_recv,
    line_send,
    line_recv,
    total_send,
    total_recv,
    gsib_send,
    gsib_recv,
    sum_send,
    sum_recv,
):
    part_count, line_count = sizes
    width, rows = tokens.shape
    depth = w_in.shape[2]
    chan = w_in.shape[1]
    wide = 2 * LANES
    chunks = rows // LANES
    low = LANES
    high = width - LANES
    modes = decay.shape[0]
    steps = rows // SUBS

    ctx = lax.axis_index("ctx")
    tp = lax.axis_index("tp")
    core = lax.rem(tp, 2)
    chip = lax.div(tp, 2)
    place = lax.rem(ctx, LINE)
    line = lax.div(ctx, LINE)
    chip_up = lax.rem(chip + 1, RING)
    chip_down = lax.rem(chip + RING - 1, RING)
    chip_far = lax.rem(chip + 2, RING)
    other = 1 - core
    up = (ctx, chip_up * 2 + core)
    down = (ctx, chip_down * 2 + core)
    sibling = (ctx, chip * 2 + other)

    def remote(src, dst, send, recv, device):
        return pltpu.make_async_remote_copy(
            src_ref=src,
            dst_ref=dst,
            send_sem=send,
            recv_sem=recv,
            device_id=device,
            device_id_type=MESH,
        )

    loads = [
        pltpu.make_async_copy(
            tokens, feat.at[pl.ds(aligned(tp * width, 16), width), :], local_sem.at[0]
        ),
        pltpu.make_async_copy(w_out, wraw.at[pl.ds(0, chan), :], local_sem.at[1]),
    ]
    for stream in range(3):
        loads.append(
            pltpu.make_async_copy(
                w_in.at[stream], win.at[stream, pl.ds(0, chan), :], local_sem.at[2 + stream]
            )
        )
    for load in loads:
        load.start()

    barrier = pltpu.get_barrier_semaphore()

    def greet(device):
        pl.semaphore_signal(barrier, inc=1, device_id=device, device_id_type=MESH)

    greet(up)
    greet(down)
    greet(sibling)
    for step in range(1, LINE):
        greet((line * LINE + lax.rem(place + step, LINE), tp))

    def greet_line(step, carry):
        greet((lax.rem(line + step, line_count) * LINE + place, tp))
        return carry

    lax.fori_loop(1, line_count, greet_line, 0)

    @pl.when(ctx > 0)
    def _():
        greet((ctx - 1, tp))

    @pl.when(ctx < part_count - 1)
    def _():
        greet((ctx + 1, tp))

    win[:, pl.ds(chan, wide - chan), :] = jnp.zeros((3, wide - chan, depth), BF16)
    taps[...] = jnp.zeros(taps.shape, F32)
    rates[...] = jnp.zeros(rates.shape, F32)
    gains[...] = jnp.zeros(gains.shape, F32)
    skips[...] = jnp.zeros(skips.shape, F32)
    rest = chan - LANES
    rates[pl.ds(0, modes), :] = decay[:, pl.ds(0, LANES)]
    rates[pl.ds(modes, modes), pl.ds(0, rest)] = decay[:, pl.ds(LANES, rest)]
    gains[pl.ds(0, modes), :] = residue[:, pl.ds(0, LANES)]
    gains[pl.ds(modes, modes), pl.ds(0, rest)] = residue[:, pl.ds(LANES, rest)]
    skips[pl.ds(0, 1), :] = skip[:, pl.ds(0, LANES)]
    skips[pl.ds(1, 1), pl.ds(0, rest)] = skip[:, pl.ds(LANES, rest)]
    for tap in range(3):
        for stream in range(3):
            row = tap * 3 + stream
            taps[pl.ds(row, 1), :] = w_short[tap, pl.ds(stream, 1), pl.ds(0, LANES)]
            taps[pl.ds(16 + row, 1), pl.ds(0, rest)] = w_short[
                tap, pl.ds(stream, 1), pl.ds(LANES, rest)
            ]
    bend = jnp.tanh(rates[...])
    gains[...] = gains[...] * jnp.sqrt(2.0 * bend / (1.0 + bend))

    wait_count = (
        3
        + (LINE - 1)
        + (line_count - 1)
        + jnp.where(ctx > 0, 1, 0)
        + jnp.where(ctx < part_count - 1, 1, 0)
    )
    pl.semaphore_wait(barrier, wait_count)

    def chunk_at(index):
        return lax.rem(index + chunks - 1, chunks)

    def block(chip_index, core_index, index, part):
        first, count = ((0, low), (low, high), (0, width))[part]
        start = (chip_index * 2 + core_index) * width + first
        return feat.at[
            pl.ds(aligned(start, 16), count),
            pl.ds(aligned(chunk_at(index) * LANES, LANES), LANES),
        ]

    def token_block(index, part):
        first, count = ((0, low), (low, high), (0, width))[part]
        return tokens.at[
            pl.ds(first, count), pl.ds(aligned(chunk_at(index) * LANES, LANES), LANES)
        ]

    def gather_copy(index, kind):
        sems = (gather_send.at[index, kind], gather_recv.at[index, kind])
        if kind < 4:
            part = kind % 2
            return remote(
                token_block(index, part),
                block(chip, core, index, part),
                *sems,
                up if kind < 2 else down,
            )
        if kind == 4:
            here = block(chip_down, core, index, 0)
            return remote(here, here, *sems, up)
        if kind == 5:
            here = block(chip_up, core, index, 1)
            return remote(here, here, *sems, down)
        if kind == 6:
            return remote(token_block(index, 2), block(chip, core, index, 2), *sems, sibling)
        whose = {7: chip_down, 8: chip_up, 9: chip_far}[kind]
        here = block(whose, core, index, 2)
        return remote(here, here, *sems, sibling)

    def gather_wait(index, kind):
        whose, owner, part = {
            0: (chip_down, core, 0),
            1: (chip_down, core, 1),
            2: (chip_up, core, 0),
            3: (chip_up, core, 1),
            4: (chip_far, core, 0),
            5: (chip_far, core, 1),
            6: (chip, other, 2),
            7: (chip_down, other, 2),
            8: (chip_up, other, 2),
            9: (chip_far, other, 2),
        }[kind]
        here = block(whose, owner, index, part)
        remote(
            here, here, gather_send.at[index, kind], gather_recv.at[index, kind], sibling
        ).wait_recv()

    def send_own(index, carry):
        for kind in (0, 3, 1, 2, 6):
            gather_copy(index, kind).start()
        return carry

    lax.fori_loop(0, chunks, send_own, 0)

    loads[1].wait()
    wraw[pl.ds(chan, wide - chan), :] = jnp.zeros((wide - chan, depth), BF16)

    def turn(index, carry):
        span = pl.ds(aligned(index * LANES, LANES), LANES)
        gmat[span, :] = jnp.broadcast_to(gain[:, span], (LANES, LANES)).T
        wturn[span, :] = wraw[:, span].astype(F32).T.astype(BF16)
        return carry

    lax.fori_loop(0, depth // LANES, turn, 0)

    def wsib_copy(index):
        return remote(
            wturn.at[pl.ds(aligned((index * 2 + other) * width, 16), width), :],
            wsib.at[pl.ds(index * width, width), :],
            wsib_send.at[index],
            wsib_recv.at[index],
            sibling,
        )

    for index in range(RING):
        wsib_copy(index).start()

    @pl.when(ctx == 0)
    def _():
        proj[:, pl.ds(0, SUBS), :] = jnp.zeros((6, SUBS, LANES), F32)

    def halo_copy():
        return remote(
            proj.at[:, pl.ds(rows, SUBS), :],
            proj.at[:, pl.ds(0, SUBS), :],
            halo_send.at[0],
            halo_recv.at[0],
            (jnp.minimum(ctx + 1, part_count - 1), tp),
        )

    def forward(index):
        gather_wait(index, 0)
        gather_copy(index, 4).start()
        gather_wait(index, 3)
        gather_copy(index, 5).start()

    def project(chunk):
        span = pl.ds(aligned(chunk * LANES, LANES), LANES)

        def square(index, total):
            value = feat[pl.ds(aligned(index * LANES, LANES), LANES), span].astype(F32)
            return total + jnp.sum((value * value).reshape(LANES // 8, 8, LANES), axis=0)

        total = lax.fori_loop(0, depth // LANES, square, jnp.zeros((8, LANES), F32))
        scale = lax.rsqrt(jnp.sum(total, axis=0, keepdims=True) / depth + 1e-06)

        def normalise(index, carry):
            here = pl.ds(aligned(index * LANES, LANES), LANES)
            value = feat[here, span].astype(F32)
            norm[here, :] = (value * scale * gmat[here, :]).astype(BF16)
            return carry

        lax.fori_loop(0, depth // LANES, normalise, 0)

        def stream_of(stream, carry):
            value = jnp.dot(win[stream], norm[...], preferred_element_type=F32)
            value = value.astype(BF16).astype(F32)
            target = pl.ds(aligned(SUBS + chunk * LANES, 8), LANES)
            for tile in range(2):
                proj[stream * 2 + tile, target, :] = value[tile * LANES : (tile + 1) * LANES].T
            return carry

        lax.fori_loop(0, 3, stream_of, 0)

    def short_mix(chunk):
        for tile in range(2):
            mixed = []
            for stream in range(3):
                piece = proj[
                    stream * 2 + tile, pl.ds(aligned(chunk * LANES, 8), LANES + SUBS), :
                ]
                value = taps[pl.ds(16 * tile + stream, 1), :] * piece[SUBS:]
                for tap in range(1, 3):
                    value = (
                        value
                        + taps[pl.ds(16 * tile + tap * 3 + stream, 1), :]
                        * piece[SUBS - tap : SUBS - tap + LANES]
                    )
                mixed.append(value)
            target = pl.ds(aligned(tile * rows + chunk * LANES, 8), LANES)
            qry[target, :] = mixed[0]
            sig[target, :] = mixed[1] * mixed[2]

    forward(0)
    for load in loads[2:]:
        load.wait()
    loads[0].wait()

    def take_chunk(index, carry):
        @pl.when(index < chunks - 1)
        def _():
            forward(index + 1)

        gather_wait(index, 1)
        gather_copy(index, 7).start()
        gather_wait(index, 2)
        gather_copy(index, 8).start()
        gather_wait(index, 4)
        gather_wait(index, 5)
        gather_copy(index, 9).start()
        for kind in (6, 7, 8, 9):
            gather_wait(index, kind)
        project(chunk_at(index))

        @pl.when((index == 0) & (ctx < part_count - 1))
        def _():
            halo_copy().start()

        @pl.when((index == 1) & (ctx > 0))
        def _():
            halo_copy().wait_recv()

        @pl.when(index > 0)
        def _():
            short_mix(chunk_at(index))

        return carry

    lax.fori_loop(0, chunks, take_chunk, 0)
    short_mix(chunks - 1)

    def advance(tile):
        keep = [
            jnp.broadcast_to(
                jnp.exp(-rates[pl.ds(tile * modes + mode, 1), :]), (SUBS, LANES)
            )
            for mode in range(modes)
        ]

        def step_of(step, states):
            value = sig[pl.ds(tile * rows + step, SUBS, stride=steps), :]
            return tuple(keep[mode] * states[mode] + value for mode in range(modes))

        states = lax.fori_loop(
            0, steps, step_of, tuple(jnp.zeros((SUBS, LANES), F32) for _ in range(modes)),
            unroll=4,
        )
        for mode in range(modes):
            ends[pl.ds((tile * modes + mode) * SUBS, SUBS), :] = states[mode]

    for tile in range(2):
        advance(tile)

    all_rates = rates[...]
    stretch_keep = jnp.exp(-all_rates * float(steps))
    block_keep = jnp.exp(-all_rates * float(rows))
    line_keep = jnp.exp(-all_rates * float(rows * LINE))

    def stretch_end(index):
        return ends[pl.ds(index, 2 * modes, stride=SUBS), :]

    state = stretch_end(0)
    for index in range(1, SUBS):
        state = stretch_keep * state + stretch_end(index)
    own_state[...] = state

    def line_copy(step):
        return remote(
            own_state,
            line_state.at[place],
            line_send.at[step],
            line_recv.at[place],
            (line * LINE + lax.rem(place + step, LINE), tp),
        )

    for step in range(1, LINE):
        line_copy(step).start()
    for step in range(1, LINE):
        source = lax.rem(place + step, LINE)
        remote(
            own_state, line_state.at[source], line_send.at[step], line_recv.at[source], sibling
        ).wait_recv()
    line_state[place] = state

    total = jnp.zeros(state.shape, F32)
    before = total
    for index in range(LINE):
        before = jnp.where(place == index, total, before)
        total = block_keep * total + line_state[index]
    line_total[...] = total

    def total_copy(step):
        return remote(
            line_total,
            totals.at[line],
            total_send.at[step],
            total_recv.at[line],
            (jnp.minimum(line + step, line_count - 1) * LINE + place, tp),
        )

    def total_start(step, carry):
        total_copy(step).start()
        return carry

    lax.fori_loop(1, line_count - line, total_start, 0)

    def total_take(index, value):
        remote(
            line_total, totals.at[index], total_send.at[0], total_recv.at[index], sibling
        ).wait_recv()
        return line_keep * value + totals[index]

    entering = lax.fori_loop(0, line, total_take, jnp.zeros(state.shape, F32))
    state = jnp.exp(-all_rates * (place * rows).astype(F32)) * entering + before
    for index in range(SUBS):
        starts[pl.ds(index * 2 * modes, 2 * modes), :] = state
        state = stretch_keep * state + stretch_end(index)

    def emit(tile):
        keep = [
            jnp.broadcast_to(
                jnp.exp(-rates[pl.ds(tile * modes + mode, 1), :]), (SUBS, LANES)
            )
            for mode in range(modes)
        ]
        scale = [
            jnp.broadcast_to(gains[pl.ds(tile * modes + mode, 1), :], (SUBS, LANES))
            for mode in range(modes)
        ]
        direct = jnp.broadcast_to(skips[pl.ds(tile, 1), :], (SUBS, LANES))

        def step_of(step, states):
            span = pl.ds(tile * rows + step, SUBS, stride=steps)
            value = sig[span, :]
            states = tuple(keep[mode] * states[mode] + value for mode in range(modes))
            terms = [scale[mode] * states[mode] for mode in range(modes)]
            while len(terms) > 1:
                terms = [terms[k] + terms[k + 1] for k in range(0, len(terms), 2)]
            gat[span, :] = qry[span, :] * (terms[0] + direct * value)
            return states

        first = tuple(
            starts[pl.ds(tile * modes + mode, SUBS, stride=2 * modes), :]
            for mode in range(modes)
        )
        lax.fori_loop(0, steps, step_of, first, unroll=2)

    for tile in range(2):
        emit(tile)

    def gsib_copy(chunk):
        span = pl.ds(aligned(chunk * LANES, LANES), LANES)
        return remote(
            gown.at[span, :], gsib.at[span, :], gsib_send.at[chunk], gsib_recv.at[chunk], sibling
        )

    def share(chunk, carry):
        span = pl.ds(aligned(chunk * LANES, LANES), LANES)
        for tile in range(2):
            gown[span, pl.ds(tile * LANES, LANES)] = gat[
                pl.ds(aligned(tile * rows + chunk * LANES, LANES), LANES), :
            ].astype(BF16)
        gsib_copy(chunk).start()
        return carry

    lax.fori_loop(0, chunks, share, 0)
    for index in range(RING):
        remote(
            wturn.at[pl.ds(0, width), :],
            wsib.at[pl.ds(index * width, width), :],
            wsib_send.at[index],
            wsib_recv.at[index],
            sibling,
        ).wait_recv()

    def partial(target, chunk):
        span = pl.ds(aligned(chunk * LANES, LANES), LANES)
        dims = (((1,), (1,)), ((), ()))
        value = lax.dot_general(
            wturn[pl.ds(aligned((target * 2 + core) * width, 16), width), :],
            gown[span, :],
            dims,
            preferred_element_type=F32,
        )
        return value + lax.dot_general(
            wsib[pl.ds(aligned(target * width, 16), width), :],
            gsib[span, :],
            dims,
            preferred_element_type=F32,
        )

    lower, upper = pl.ds(0, low), pl.ds(low, high)

    def sum_copy(chunk, kind):
        source, target, part, device = (
            (far_out, far_in, lower, up),
            (far_out, far_in, upper, down),
            (up_out, up_in, upper, up),
            (down_out, down_in, lower, down),
            (up_out, up_in, lower, up),
            (down_out, down_in, upper, down),
        )[kind]
        return remote(
            source.at[chunk, part, :],
            target.at[chunk, part, :],
            sum_send.at[chunk, kind],
            sum_recv.at[chunk, kind],
            device,
        )

    def send_far(chunk, carry):
        gsib_copy(chunk).wait_recv()
        far_out[chunk] = partial(chip_far, chunk).astype(BF16)
        sum_copy(chunk, 0).start()
        sum_copy(chunk, 1).start()
        return carry

    lax.fori_loop(0, chunks, send_far, 0)

    def send_near(chunk, carry):
        value = partial(chip_up, chunk)
        up_out[chunk, upper, :] = value[low:].astype(BF16)
        sum_copy(chunk, 2).start()
        held[chunk, lower, :] = value[:low]
        value = partial(chip_down, chunk)
        down_out[chunk, lower, :] = value[:low].astype(BF16)
        sum_copy(chunk, 3).start()
        held[chunk, upper, :] = value[low:]
        return carry

    lax.fori_loop(0, chunks, send_near, 0)

    def send_sums(chunk, carry):
        sum_copy(chunk, 0).wait_recv()
        up_out[chunk, lower, :] = (
            held[chunk, lower, :] + far_in[chunk, lower, :].astype(F32)
        ).astype(BF16)
        sum_copy(chunk, 4).start()
        sum_copy(chunk, 1).wait_recv()
        down_out[chunk, upper, :] = (
            held[chunk, upper, :] + far_in[chunk, upper, :].astype(F32)
        ).astype(BF16)
        sum_copy(chunk, 5).start()
        mine[chunk] = partial(chip, chunk)
        return carry

    lax.fori_loop(0, chunks, send_sums, 0)

    def finish(chunk, carry):
        for kind in range(2, 6):
            sum_copy(chunk, kind).wait_recv()
        value = mine[chunk] + up_in[chunk].astype(F32) + down_in[chunk].astype(F32)
        out[:, pl.ds(aligned(chunk * LANES, LANES), LANES)] = value.astype(BF16)
        return carry

    lax.fori_loop(0, chunks, finish, 0)

    def drain(index, carry):
        for kind in range(10):
            gather_copy(index, kind).wait_send()
        for kind in range(6):
            sum_copy(index, kind).wait_send()
        gsib_copy(index).wait_send()
        return carry

    lax.fori_loop(0, chunks, drain, 0)
    for index in range(RING):
        wsib_copy(index).wait_send()
    for step in range(1, LINE):
        line_copy(step).wait_send()

    def total_drain(step, carry):
        total_copy(step).wait_send()
        return carry

    lax.fori_loop(1, line_count - line, total_drain, 0)

    @pl.when(ctx < part_count - 1)
    def _():
        halo_copy().wait_send()


def solution(mesh):
    part_count = mesh.shape["ctx"]
    line_count = part_count // LINE

    def body(tokens, norm_gain, w_in, w_short, decay_rate, residue, skip_gain, w_out):
        width, rows = tokens.shape
        chan, depth = w_in.shape[1:]
        modes = decay_rate.shape[0]
        chunks = rows // LANES
        wide = 2 * LANES
        vmem = pltpu.VMEM
        dma = pltpu.SemaphoreType.DMA
        hbm = pl.BlockSpec(memory_space=pl.ANY)
        near = pl.BlockSpec(memory_space=pltpu.VMEM)
        scratch = [
            vmem((depth, rows), BF16),
            vmem((3, wide, depth), BF16),
            vmem((depth, LANES), F32),
            vmem((depth, LANES), BF16),
            vmem((6, SUBS + rows, LANES), F32),
            vmem((2 * rows, LANES), F32),
            vmem((2 * rows, LANES), F32),
            vmem((2 * rows, LANES), F32),
            vmem((32, LANES), F32),
            vmem((2 * modes, LANES), F32),
            vmem((2 * modes, LANES), F32),
            vmem((8, LANES), F32),
            vmem((2 * modes * SUBS, LANES), F32),
            vmem((2 * modes * SUBS, LANES), F32),
            vmem((2 * modes, LANES), F32),
            vmem((LINE, 2 * modes, LANES), F32),
            vmem((2 * modes, LANES), F32),
            vmem((line_count, 2 * modes, LANES), F32),
            vmem((wide, depth), BF16),
            vmem((depth, wide), BF16),
            vmem((RING * width, wide), BF16),
            vmem((rows, wide), BF16),
            vmem((rows, wide), BF16),
            vmem((chunks, width, LANES), BF16),
            vmem((chunks, width, LANES), BF16),
            vmem((chunks, width, LANES), BF16),
            vmem((chunks, width, LANES), BF16),
            vmem((chunks, width, LANES), BF16),
            vmem((chunks, width, LANES), BF16),
            vmem((chunks, width, LANES), F32),
            vmem((chunks, width, LANES), F32),
            dma((5,)),
            dma((chunks, 10)),
            dma((chunks, 10)),
            dma((1,)),
            dma((1,)),
            dma((RING,)),
            dma((RING,)),
            dma((LINE,)),
            dma((LINE,)),
            dma((line_count,)),
            dma((line_count,)),
            dma((chunks,)),
            dma((chunks,)),
            dma((chunks, 6)),
            dma((chunks, 6)),
        ]
        return pl.pallas_call(
            functools.partial(mixer_kernel, (part_count, line_count)),
            out_shape=jax.ShapeDtypeStruct((width, rows), BF16),
            in_specs=[hbm, near, hbm, near, near, near, near, hbm],
            out_specs=near,
            scratch_shapes=scratch,
            compiler_params=pltpu.CompilerParams(collective_id=0, has_side_effects=True),
        )(
            tokens,
            norm_gain[None, :],
            w_in,
            w_short,
            decay_rate,
            residue,
            skip_gain[None, :],
            w_out,
        )

    placed = (
        P("tp", "ctx"),
        P(),
        P(None, "tp", None),
        P(None, None, "tp"),
        P(None, "tp"),
        P(None, "tp"),
        P("tp"),
        P("tp", None),
    )
    return jax.shard_map(
        body, mesh=mesh, in_specs=placed, out_specs=P("tp", "ctx"), check_vma=False
    )
```

```python
import functools

import jax
import jax.numpy as jnp
from jax import lax
from jax.experimental import pallas as pl
from jax.experimental.pallas import tpu as pltpu
from jax.sharding import PartitionSpec as P

MESH = pl.DeviceIdType.MESH
F32 = jnp.float32
BF16 = jnp.bfloat16
RING = 4
LINE = 4
LANES = 128
SUBS = 8


def aligned(value, step):
    return pl.multiple_of(value, step)


def mixer_kernel(
    sizes,
    tokens,
    gain_ref,
    w_in,
    short_ref,
    decay_ref,
    residue_ref,
    skip_ref,
    w_out,
    out,
    gain,
    w_short,
    decay,
    residue,
    skip,
    feat,
    win,
    gmat,
    norm,
    proj,
    sig,
    qry,
    gat,
    taps,
    rates,
    gains,
    skips,
    ends,
    starts,
    lead,
    keep_one,
    keep_eight,
    wide_gain,
    chunk_end,
    enter,
    own_state,
    line_state,
    line_total,
    totals,
    wraw,
    wturn,
    wsib,
    gown,
    gsib,
    far_out,
    far_in,
    up_out,
    up_in,
    down_out,
    down_in,
    held,
    mine,
    local_sem,
    gather_send,
    gather_recv,
    halo_send,
    halo_recv,
    wsib_send,
    wsib_recv,
    line_send,
    line_recv,
    total_send,
    total_recv,
    gsib_send,
    gsib_recv,
    sum_send,
    sum_recv,
):
    part_count, line_count = sizes
    width, rows = tokens.shape
    depth = w_in.shape[2]
    chan = w_in.shape[1]
    wide = 2 * LANES
    chunks = rows // LANES
    low = LANES
    high = width - LANES
    modes = decay_ref.shape[0]
    steps = LANES // SUBS

    ctx = lax.axis_index("ctx")
    tp = lax.axis_index("tp")
    core = lax.rem(tp, 2)
    chip = lax.div(tp, 2)
    place = lax.rem(ctx, LINE)
    line = lax.div(ctx, LINE)
    chip_up = lax.rem(chip + 1, RING)
    chip_down = lax.rem(chip + RING - 1, RING)
    chip_far = lax.rem(chip + 2, RING)
    other = 1 - core
    up = (ctx, chip_up * 2 + core)
    down = (ctx, chip_down * 2 + core)
    sibling = (ctx, chip * 2 + other)

    def remote(src, dst, send, recv, device):
        return pltpu.make_async_remote_copy(
            src_ref=src,
            dst_ref=dst,
            send_sem=send,
            recv_sem=recv,
            device_id=device,
            device_id_type=MESH,
        )

    barrier = pltpu.get_barrier_semaphore()

    def greet(device):
        pl.semaphore_signal(barrier, inc=1, device_id=device, device_id_type=MESH)

    greet(up)
    greet(down)
    greet(sibling)
    for step in range(1, LINE):
        greet((line * LINE + lax.rem(place + step, LINE), tp))

    def greet_line(step, carry):
        greet((lax.rem(line + step, line_count) * LINE + place, tp))
        return carry

    lax.fori_loop(1, line_count, greet_line, 0)

    @pl.when(ctx > 0)
    def _():
        greet((ctx - 1, tp))

    @pl.when(ctx < part_count - 1)
    def _():
        greet((ctx + 1, tp))

    loads = [
        pltpu.make_async_copy(
            tokens, feat.at[pl.ds(aligned(tp * width, 16), width), :], local_sem.at[0]
        ),
        pltpu.make_async_copy(w_out, wraw.at[pl.ds(0, chan), :], local_sem.at[1]),
    ]
    for stream in range(3):
        loads.append(
            pltpu.make_async_copy(
                w_in.at[stream], win.at[pl.ds(stream * wide, chan), :], local_sem.at[2 + stream]
            )
        )
    small = [
        pltpu.make_async_copy(source, target, local_sem.at[5 + index])
        for index, (source, target) in enumerate(
            (
                (decay_ref, decay),
                (residue_ref, residue),
                (short_ref, w_short),
                (skip_ref, skip),
                (gain_ref, gain),
            )
        )
    ]
    for load in small + loads:
        load.start()

    for stream in range(3):
        win[pl.ds(stream * wide + chan, wide - chan), :] = jnp.zeros((wide - chan, depth), BF16)
    taps[...] = jnp.zeros(taps.shape, F32)
    rates[...] = jnp.zeros(rates.shape, F32)
    gains[...] = jnp.zeros(gains.shape, F32)
    skips[...] = jnp.zeros(skips.shape, F32)
    rest = chan - LANES
    for load in small:
        load.wait()
    rates[pl.ds(0, modes), :] = decay[:, pl.ds(0, LANES)]
    rates[pl.ds(modes, modes), pl.ds(0, rest)] = decay[:, pl.ds(LANES, rest)]
    gains[pl.ds(0, modes), :] = residue[:, pl.ds(0, LANES)]
    gains[pl.ds(modes, modes), pl.ds(0, rest)] = residue[:, pl.ds(LANES, rest)]
    skips[pl.ds(0, 1), :] = skip[:, pl.ds(0, LANES)]
    skips[pl.ds(1, 1), pl.ds(0, rest)] = skip[:, pl.ds(LANES, rest)]
    for tap in range(3):
        for stream in range(3):
            row = tap * 3 + stream
            taps[pl.ds(row, 1), :] = w_short[tap, pl.ds(stream, 1), pl.ds(0, LANES)]
            taps[pl.ds(16 + row, 1), pl.ds(0, rest)] = w_short[
                tap, pl.ds(stream, 1), pl.ds(LANES, rest)
            ]
    bend = jnp.tanh(rates[...])
    gains[...] = gains[...] * jnp.sqrt(2.0 * bend / (1.0 + bend))

    wait_count = (
        3
        + (LINE - 1)
        + (line_count - 1)
        + jnp.where(ctx > 0, 1, 0)
        + jnp.where(ctx < part_count - 1, 1, 0)
    )
    pl.semaphore_wait(barrier, wait_count)

    def chunk_at(index):
        return lax.rem(index + chunks - 1, chunks)

    def block(chip_index, core_index, index, part):
        first, count = ((0, low), (low, high), (0, width))[part]
        start = (chip_index * 2 + core_index) * width + first
        return feat.at[
            pl.ds(aligned(start, 16), count),
            pl.ds(aligned(chunk_at(index) * LANES, LANES), LANES),
        ]

    def token_block(index, part):
        first, count = ((0, low), (low, high), (0, width))[part]
        return tokens.at[
            pl.ds(first, count), pl.ds(aligned(chunk_at(index) * LANES, LANES), LANES)
        ]

    def gather_copy(index, kind):
        sems = (gather_send.at[index, kind], gather_recv.at[index, kind])
        if kind < 4:
            part = kind % 2
            return remote(
                token_block(index, part),
                block(chip, core, index, part),
                *sems,
                up if kind < 2 else down,
            )
        if kind == 4:
            here = block(chip_down, core, index, 0)
            return remote(here, here, *sems, up)
        if kind == 5:
            here = block(chip_up, core, index, 1)
            return remote(here, here, *sems, down)
        if kind == 6:
            return remote(token_block(index, 2), block(chip, core, index, 2), *sems, sibling)
        whose = {7: chip_down, 8: chip_up, 9: chip_far}[kind]
        here = block(whose, core, index, 2)
        return remote(here, here, *sems, sibling)

    def gather_wait(index, kind):
        whose, owner, part = {
            0: (chip_down, core, 0),
            1: (chip_down, core, 1),
            2: (chip_up, core, 0),
            3: (chip_up, core, 1),
            4: (chip_far, core, 0),
            5: (chip_far, core, 1),
            6: (chip, other, 2),
            7: (chip_down, other, 2),
            8: (chip_up, other, 2),
            9: (chip_far, other, 2),
        }[kind]
        here = block(whose, owner, index, part)
        remote(
            here, here, gather_send.at[index, kind], gather_recv.at[index, kind], sibling
        ).wait_recv()

    def send_own(index, carry):
        for kind in (0, 3):
            gather_copy(index, kind).start()
        return carry

    def send_rest(index, carry):
        for kind in (1, 2):
            gather_copy(index, kind).start()
        return carry

    def send_sibling(index, carry):
        gather_copy(index, 6).start()
        return carry

    lax.fori_loop(0, chunks, send_own, 0)
    send_rest(0, 0)
    lax.fori_loop(0, chunks, send_sibling, 0)

    loads[1].wait()
    wraw[pl.ds(chan, wide - chan), :] = jnp.zeros((wide - chan, depth), BF16)

    def turn(index, carry):
        span = pl.ds(aligned(index * LANES, LANES), LANES)
        gmat[span, :] = jnp.broadcast_to(gain[pl.ds(index, 1), :], (LANES, LANES)).T
        wturn[span, :] = wraw[:, span].astype(F32).T.astype(BF16)
        return carry

    lax.fori_loop(0, depth // LANES, turn, 0)

    def wsib_copy(index):
        return remote(
            wturn.at[pl.ds(aligned((index * 2 + other) * width, 16), width), :],
            wsib.at[pl.ds(index * width, width), :],
            wsib_send.at[index],
            wsib_recv.at[index],
            sibling,
        )

    for index in range(RING):
        wsib_copy(index).start()

    @pl.when(ctx == 0)
    def _():
        proj[:, pl.ds(0, SUBS), :] = jnp.zeros((6, SUBS, LANES), F32)

    def halo_copy():
        return remote(
            proj.at[:, pl.ds(rows, SUBS), :],
            proj.at[:, pl.ds(0, SUBS), :],
            halo_send.at[0],
            halo_recv.at[0],
            (jnp.minimum(ctx + 1, part_count - 1), tp),
        )

    def forward(index):
        gather_wait(index, 0)
        gather_copy(index, 4).start()
        gather_wait(index, 3)
        gather_copy(index, 5).start()

    def project(chunk):
        span = pl.ds(aligned(chunk * LANES, LANES), LANES)

        def square(index, total):
            value = feat[pl.ds(aligned(index * LANES, LANES), LANES), span].astype(F32)
            return total + jnp.sum((value * value).reshape(LANES // 8, 8, LANES), axis=0)

        total = lax.fori_loop(0, depth // LANES, square, jnp.zeros((8, LANES), F32))
        scale = lax.rsqrt(jnp.sum(total, axis=0, keepdims=True) / depth + 1e-06)

        def normalise(index, carry):
            here = pl.ds(aligned(index * LANES, LANES), LANES)
            value = feat[here, span].astype(F32)
            norm[here, :] = (value * scale * gmat[here, :]).astype(BF16)
            return carry

        lax.fori_loop(0, depth // LANES, normalise, 0)

        value = jnp.dot(win[...], norm[...], preferred_element_type=F32)
        value = value.astype(BF16).astype(F32)
        target = pl.ds(aligned(SUBS + chunk * LANES, 8), LANES)
        for tile in range(6):
            proj[tile, target, :] = value[tile * LANES : (tile + 1) * LANES].T

    def short_mix(chunk):
        for tile in range(2):
            mixed = []
            for stream in range(3):
                piece = proj[
                    stream * 2 + tile, pl.ds(aligned(chunk * LANES, 8), LANES + SUBS), :
                ]
                value = taps[pl.ds(16 * tile + stream, 1), :] * piece[SUBS:]
                for tap in range(1, 3):
                    value = (
                        value
                        + taps[pl.ds(16 * tile + tap * 3 + stream, 1), :]
                        * piece[SUBS - tap : SUBS - tap + LANES]
                    )
                mixed.append(value)
            target = pl.ds(aligned(tile * rows + chunk * LANES, 8), LANES)
            qry[target, :] = mixed[0]
            sig[target, :] = mixed[1] * mixed[2]

    for load in loads[2:]:
        load.wait()
    loads[0].wait()
    for index in range(RING):
        remote(
            wturn.at[pl.ds(0, width), :],
            wsib.at[pl.ds(index * width, width), :],
            wsib_send.at[index],
            wsib_recv.at[index],
            sibling,
        ).wait_recv()
    ahead = (lax.broadcasted_iota(jnp.int32, (SUBS, LANES), 0) + 1).astype(F32)
    for row in range(2 * modes):
        span = pl.ds(row * SUBS, SUBS)
        rate = jnp.broadcast_to(rates[pl.ds(row, 1), :], (SUBS, LANES))
        wide_gain[span, :] = jnp.broadcast_to(gains[pl.ds(row, 1), :], (SUBS, LANES))
        lead[span, :] = wide_gain[span, :] * jnp.exp(-rate * ahead)
        keep_one[span, :] = jnp.exp(-rate)
        keep_eight[span, :] = jnp.exp(-rate * float(SUBS))

    all_rates = rates[...]
    stretch_keep = jnp.exp(-all_rates * float(steps))
    chunk_keep = jnp.exp(-all_rates * float(LANES))
    block_keep = jnp.exp(-all_rates * float(rows))
    line_keep = jnp.exp(-all_rates * float(rows * LINE))

    def mode_rows(tile):
        return [pl.ds((tile * modes + mode) * SUBS, SUBS) for mode in range(modes)]

    def advance(chunk):
        for tile in range(2):
            spans = mode_rows(tile)
            keep = [keep_one[span, :] for span in spans]

            def step_of(step, states):
                value = sig[pl.ds(tile * rows + chunk * LANES + step, SUBS, stride=steps), :]
                return tuple(keep[mode] * states[mode] + value for mode in range(modes))

            states = lax.fori_loop(
                0,
                steps,
                step_of,
                tuple(jnp.zeros((SUBS, LANES), F32) for _ in range(modes)),
                unroll=4,
            )
            for span, state in zip(spans, states):
                ends[span, :] = state
        inner = jnp.zeros((2 * modes, LANES), F32)
        for index in range(SUBS):
            starts[chunk, pl.ds(index * 2 * modes, 2 * modes), :] = inner
            inner = stretch_keep * inner + ends[pl.ds(index, 2 * modes, stride=SUBS), :]
        chunk_end[chunk] = inner

    def emit(chunk, carry):
        for tile in range(2):
            spans = mode_rows(tile)
            keep = [keep_one[span, :] for span in spans]
            scale = [wide_gain[span, :] for span in spans]
            direct = jnp.broadcast_to(skips[pl.ds(tile, 1), :], (SUBS, LANES))

            def step_of(step, states):
                span = pl.ds(tile * rows + chunk * LANES + step, SUBS, stride=steps)
                value = sig[span, :]
                states = tuple(keep[mode] * states[mode] + value for mode in range(modes))
                terms = [scale[mode] * states[mode] for mode in range(modes)]
                while len(terms) > 1:
                    terms = [terms[k] + terms[k + 1] for k in range(0, len(terms), 2)]
                gat[span, :] = terms[0] + direct * value
                return states

            first = tuple(
                starts[chunk, pl.ds(tile * modes + mode, SUBS, stride=2 * modes), :]
                for mode in range(modes)
            )
            lax.fori_loop(0, steps, step_of, first, unroll=2)
        return carry

    def pass_near(index, carry):
        gather_wait(index, 1)
        gather_copy(index, 7).start()
        gather_wait(index, 2)
        gather_copy(index, 8).start()
        return carry

    def take_far(index):
        gather_wait(index, 4)
        gather_wait(index, 5)
        gather_copy(index, 9).start()
        for kind in (6, 7, 8, 9):
            gather_wait(index, kind)
        project(chunk_at(index))

    forward(0)
    send_rest(1, 0)
    forward(1)
    send_rest(2, 0)
    send_rest(3, 0)
    forward(2)
    pass_near(0, 0)
    take_far(0)

    @pl.when(ctx < part_count - 1)
    def _():
        halo_copy().start()

    forward(3)
    lax.fori_loop(1, chunks, pass_near, 0)

    def take_chunk(index, carry):
        take_far(index)

        @pl.when((index == 1) & (ctx > 0))
        def _():
            halo_copy().wait_recv()

        short_mix(chunk_at(index))
        advance(chunk_at(index))
        return carry

    lax.fori_loop(1, chunks, take_chunk, 0)
    short_mix(chunks - 1)
    advance(chunks - 1)

    state = chunk_end[0]
    for chunk in range(1, chunks):
        state = chunk_keep * state + chunk_end[chunk]
    own_state[...] = state

    def line_copy(step):
        return remote(
            own_state,
            line_state.at[place],
            line_send.at[step],
            line_recv.at[place],
            (line * LINE + lax.rem(place + step, LINE), tp),
        )

    for step in range(1, LINE):
        line_copy(step).start()

    lax.fori_loop(0, 2, emit, 0)
    for step in range(1, LINE):
        source = lax.rem(place + step, LINE)
        remote(
            own_state, line_state.at[source], line_send.at[step], line_recv.at[source], sibling
        ).wait_recv()
    line_state[place] = state

    total = jnp.zeros(state.shape, F32)
    before = total
    for index in range(LINE):
        before = jnp.where(place == index, total, before)
        total = block_keep * total + line_state[index]
    line_total[...] = total

    def total_copy(step):
        return remote(
            line_total,
            totals.at[line],
            total_send.at[step],
            total_recv.at[line],
            (jnp.minimum(line + step, line_count - 1) * LINE + place, tp),
        )

    def total_start(step, carry):
        total_copy(step).start()
        return carry

    lax.fori_loop(1, line_count - line, total_start, 0)
    lax.fori_loop(2, chunks, emit, 0)

    def total_take(index, value):
        remote(
            line_total, totals.at[index], total_send.at[0], total_recv.at[index], sibling
        ).wait_recv()
        return line_keep * value + totals[index]

    entering = lax.fori_loop(0, line, total_take, jnp.zeros(state.shape, F32))
    state = jnp.exp(-all_rates * (place * rows).astype(F32)) * entering + before
    for chunk in range(chunks):
        enter[chunk] = state
        state = chunk_keep * state + chunk_end[chunk]

    def complete(chunk, tile):
        spans = mode_rows(tile)
        keep = [keep_eight[span, :] for span in spans]
        base = chunk * LANES

        def step_of(step, values):
            halves = []
            for half in range(2):
                terms = list(values)
                while len(terms) > 1:
                    terms = [terms[k] + terms[k + 1] for k in range(0, len(terms), 2)]
                span = pl.ds(
                    aligned(tile * rows + base + step * 2 * SUBS + half * SUBS, SUBS), SUBS
                )
                halves.append(qry[span, :] * (gat[span, :] + terms[0]))
                values = tuple(keep[mode] * values[mode] for mode in range(modes))
            gown[
                pl.ds(aligned(base + step * 2 * SUBS, 2 * SUBS), 2 * SUBS),
                pl.ds(tile * LANES, LANES),
            ] = jnp.concatenate(halves, axis=0).astype(BF16)
            return values

        values = tuple(
            lead[spans[mode], :] * enter[chunk, pl.ds(tile * modes + mode, 1), :]
            for mode in range(modes)
        )
        lax.fori_loop(0, LANES // (2 * SUBS), step_of, values)

    def gsib_copy(chunk):
        span = pl.ds(aligned(chunk * LANES, LANES), LANES)
        return remote(
            gown.at[span, :], gsib.at[span, :], gsib_send.at[chunk], gsib_recv.at[chunk], sibling
        )

    def partial(target, chunk):
        span = pl.ds(aligned(chunk * LANES, LANES), LANES)
        dims = (((1,), (1,)), ((), ()))
        value = lax.dot_general(
            wturn[pl.ds(aligned((target * 2 + core) * width, 16), width), :],
            gown[span, :],
            dims,
            preferred_element_type=F32,
        )
        return value + lax.dot_general(
            wsib[pl.ds(aligned(target * width, 16), width), :],
            gsib[span, :],
            dims,
            preferred_element_type=F32,
        )

    lower, upper = pl.ds(0, low), pl.ds(low, high)

    def sum_copy(chunk, kind):
        source, target, part, device = (
            (far_out, far_in, lower, up),
            (far_out, far_in, upper, down),
            (up_out, up_in, upper, up),
            (down_out, down_in, lower, down),
            (up_out, up_in, lower, up),
            (down_out, down_in, upper, down),
        )[kind]
        return remote(
            source.at[chunk, part, :],
            target.at[chunk, part, :],
            sum_send.at[chunk, kind],
            sum_recv.at[chunk, kind],
            device,
        )

    def send_far(chunk, carry):
        gsib_copy(chunk).wait_recv()
        far_out[chunk] = partial(chip_far, chunk).astype(BF16)
        sum_copy(chunk, 0).start()
        sum_copy(chunk, 1).start()
        return carry

    def share(chunk, carry):
        for tile in range(2):
            complete(chunk, tile)
        gsib_copy(chunk).start()

        @pl.when(chunk > 0)
        def _():
            send_far(chunk - 1, 0)

        return carry

    lax.fori_loop(0, chunks, share, 0)
    send_far(chunks - 1, 0)

    def send_near(chunk, carry):
        value = partial(chip_up, chunk)
        up_out[chunk, upper, :] = value[low:].astype(BF16)
        sum_copy(chunk, 2).start()
        held[chunk, lower, :] = value[:low]
        value = partial(chip_down, chunk)
        down_out[chunk, lower, :] = value[:low].astype(BF16)
        sum_copy(chunk, 3).start()
        held[chunk, upper, :] = value[low:]
        return carry

    lax.fori_loop(0, chunks, send_near, 0)

    def send_sums(chunk, carry):
        sum_copy(chunk, 0).wait_recv()
        up_out[chunk, lower, :] = (
            held[chunk, lower, :] + far_in[chunk, lower, :].astype(F32)
        ).astype(BF16)
        sum_copy(chunk, 4).start()
        sum_copy(chunk, 1).wait_recv()
        down_out[chunk, upper, :] = (
            held[chunk, upper, :] + far_in[chunk, upper, :].astype(F32)
        ).astype(BF16)
        sum_copy(chunk, 5).start()
        mine[chunk] = partial(chip, chunk)
        return carry

    lax.fori_loop(0, chunks, send_sums, 0)

    def finish(chunk, carry):
        for kind in range(2, 6):
            sum_copy(chunk, kind).wait_recv()
        value = mine[chunk] + up_in[chunk].astype(F32) + down_in[chunk].astype(F32)
        out[:, pl.ds(aligned(chunk * LANES, LANES), LANES)] = value.astype(BF16)
        return carry

    lax.fori_loop(0, chunks, finish, 0)

    def drain(index, carry):
        for kind in range(10):
            gather_copy(index, kind).wait_send()
        for kind in range(6):
            sum_copy(index, kind).wait_send()
        gsib_copy(index).wait_send()
        return carry

    lax.fori_loop(0, chunks, drain, 0)
    for index in range(RING):
        wsib_copy(index).wait_send()
    for step in range(1, LINE):
        line_copy(step).wait_send()

    def total_drain(step, carry):
        total_copy(step).wait_send()
        return carry

    lax.fori_loop(1, line_count - line, total_drain, 0)

    @pl.when(ctx < part_count - 1)
    def _():
        halo_copy().wait_send()


def solution(mesh):
    part_count = mesh.shape["ctx"]
    line_count = part_count // LINE

    def body(tokens, norm_gain, w_in, w_short, decay_rate, residue, skip_gain, w_out):
        width, rows = tokens.shape
        chan, depth = w_in.shape[1:]
        modes = decay_rate.shape[0]
        chunks = rows // LANES
        wide = 2 * LANES
        vmem = pltpu.VMEM
        dma = pltpu.SemaphoreType.DMA
        hbm = pl.BlockSpec(memory_space=pl.ANY)
        near = pl.BlockSpec(memory_space=pltpu.VMEM)
        scratch = [
            vmem((depth // LANES, LANES), F32),
            vmem(w_short.shape, F32),
            vmem(decay_rate.shape, F32),
            vmem(residue.shape, F32),
            vmem((1, chan), F32),
            vmem((depth, rows), BF16),
            vmem((3 * wide, depth), BF16),
            vmem((depth, LANES), F32),
            vmem((depth, LANES), BF16),
            vmem((6, SUBS + rows, LANES), F32),
            vmem((2 * rows, LANES), F32),
            vmem((2 * rows, LANES), F32),
            vmem((2 * rows, LANES), F32),
            vmem((32, LANES), F32),
            vmem((2 * modes, LANES), F32),
            vmem((2 * modes, LANES), F32),
            vmem((8, LANES), F32),
            vmem((2 * modes * SUBS, LANES), F32),
            vmem((chunks, 2 * modes * SUBS, LANES), F32),
            vmem((2 * modes * SUBS, LANES), F32),
            vmem((2 * modes * SUBS, LANES), F32),
            vmem((2 * modes * SUBS, LANES), F32),
            vmem((2 * modes * SUBS, LANES), F32),
            vmem((chunks, 2 * modes, LANES), F32),
            vmem((chunks, 2 * modes, LANES), F32),
            vmem((2 * modes, LANES), F32),
            vmem((LINE, 2 * modes, LANES), F32),
            vmem((2 * modes, LANES), F32),
            vmem((line_count, 2 * modes, LANES), F32),
            vmem((wide, depth), BF16),
            vmem((depth, wide), BF16),
            vmem((RING * width, wide), BF16),
            vmem((rows, wide), BF16),
            vmem((rows, wide), BF16),
            vmem((chunks, width, LANES), BF16),
            vmem((chunks, width, LANES), BF16),
            vmem((chunks, width, LANES), BF16),
            vmem((chunks, width, LANES), BF16),
            vmem((chunks, width, LANES), BF16),
            vmem((chunks, width, LANES), BF16),
            vmem((chunks, width, LANES), F32),
            vmem((chunks, width, LANES), F32),
            dma((10,)),
            dma((chunks, 10)),
            dma((chunks, 10)),
            dma((1,)),
            dma((1,)),
            dma((RING,)),
            dma((RING,)),
            dma((LINE,)),
            dma((LINE,)),
            dma((line_count,)),
            dma((line_count,)),
            dma((chunks,)),
            dma((chunks,)),
            dma((chunks, 6)),
            dma((chunks, 6)),
        ]
        return pl.pallas_call(
            functools.partial(mixer_kernel, (part_count, line_count)),
            out_shape=jax.ShapeDtypeStruct((width, rows), BF16),
            in_specs=[hbm] * 8,
            out_specs=near,
            scratch_shapes=scratch,
            compiler_params=pltpu.CompilerParams(collective_id=0, has_side_effects=True),
        )(
            tokens,
            norm_gain.reshape(depth // LANES, LANES),
            w_in,
            w_short,
            decay_rate,
            residue,
            skip_gain[None, :],
            w_out,
        )

    placed = (
        P("tp", "ctx"),
        P(),
        P(None, "tp", None),
        P(None, None, "tp"),
        P(None, "tp"),
        P(None, "tp"),
        P("tp"),
        P("tp", None),
    )
    return jax.shard_map(
        body, mesh=mesh, in_specs=placed, out_specs=P("tp", "ctx"), check_vma=False
    )
```
